512 devices in a mesh: cuts: 128 (over z, x, core), stem: 4 (over y).
Axes of the slice: x: 4, y: 4, z: 16, core: 2. Of those that a mesh axis runs over, the one named last changes fastest.
Arguments:
- stem_tensor: bfloat16 [8, 64, 1024], P('stem'), may hold values from -6 to 6
- mid_tensors: bfloat16 [8192, 512, 128], P(('cuts', 'stem')), may hold values from -0.1875 to 0.1875
- right_tensors: bfloat16 [8, 8192, 64, 128], P(None, ('cuts', 'stem')), may hold values from -0.001953125 to 0.001953125
Outputs:
- amplitudes: float32 [8192], P('cuts')
The draws below stay inside these ranges and needn't reach their ends.
All inputs are finite; a program needn't handle non-finite values.
Results may differ from the reference program's by a relative error of at most 0.0029.
Values may be sent and summed in bfloat16 or wider, within the bound.
A program may use at most 64 MiB of HBM per device.

```python
import jax
import jax.numpy as jnp
from jax import lax

A = 64
B = 64
K = 512
R = 64
C = 8
MT = 16
BRANCHES = 8192
TERMS = 8388608


def block_scale(stream_key, shape, shards, smallest, high):
    gain, own = 1.0, jax.random.fold_in(stream_key, 6)
    for axis_at, shards_of in shards:
        heights = jnp.exp(jax.random.uniform(jax.random.fold_in(own, axis_at), (shards_of,), jnp.float32, smallest / len(shards), high / len(shards)))
        gain = gain * jnp.repeat(heights, shape[axis_at] // shards_of).reshape([-1 if axis == axis_at else 1 for axis in range(len(shape))])
    return gain


def bell_draw(own_key, dims, width, limit, split=(), held_as=jnp.bfloat16):
    level = block_scale(own_key, dims, split, -0.22, 0.18) if split else 1.0
    array = jax.random.normal(own_key, dims, jnp.float32) * width * level
    return jnp.minimum(jnp.maximum(array, -limit), limit).astype(held_as)


def setup_inputs(seed: int = 0) -> dict:
    key_of = jax.random.split(jax.random.key(seed), 4)
    return {
        "stem_tensor": bell_draw(key_of[0], (C, A, 2 * K), 1.0, 6.0, ((0, 4),)),
        "mid_tensors": bell_draw(key_of[1], (BRANCHES, K, 2 * R), (2 * K) ** -0.5, 0.1875, ((0, 512),)),
        "right_tensors": bell_draw(key_of[2], (C, BRANCHES, R, 2 * B), TERMS ** -0.5, 0.001953125, ((1, 512),)),
    }


def widen(tensor):
    half_width = tensor.shape[-1] // 2
    real_part = tensor[..., :half_width]
    imag_part = tensor[..., half_width:]
    upper_rows = jnp.concatenate([real_part, imag_part], axis=-1)
    lower_rows = jnp.concatenate([-imag_part, real_part], axis=-1)
    return jnp.concatenate([upper_rows, lower_rows], axis=-2)


def reference(stem_tensor, mid_tensors, right_tensors):
    group_count = mid_tensors.shape[0] // MT
    stem_rows = stem_tensor.reshape(C * A, 2 * K)
    mid_groups = mid_tensors.reshape(group_count, MT, K, 2 * R)
    right_groups = jnp.moveaxis(right_tensors.reshape(C, group_count, MT, R, 2 * B), 1, 0)

    def accumulate(running, paired):
        mid_block, right_block = paired
        widened = jnp.moveaxis(widen(mid_block), 0, 1).reshape(2 * K, MT * 2 * R)
        first_step = jnp.dot(stem_rows, widened, preferred_element_type=jnp.float32).astype(jnp.bfloat16)
        first_step = lax.optimization_barrier(first_step).astype(jnp.float32).reshape(C, A, MT * 2 * R)
        right_wide = widen(right_block).reshape(C, MT * 2 * R, 2 * B).astype(jnp.float32)
        update = jnp.einsum("iaq,iqb->ab", first_step, right_wide, precision=lax.Precision.HIGHEST)
        return running + update, None

    running, _ = lax.scan(accumulate, jnp.zeros((A, 2 * B), jnp.float32), (mid_groups, right_groups))
    return running.reshape(2 * A * B)
```

```python
import functools

import jax
import jax.numpy as jnp
from jax import lax
from jax.experimental import pallas as pl
from jax.experimental.pallas import tpu as pltpu
from jax.sharding import PartitionSpec as P

MESH = pl.DeviceIdType.MESH
NX = 4
NCORE = 2


def kernel(
    nz, ny,
    stem_hbm, mid_hbm, right_hbm, out_ref,
    stem_v, mid_v, right_v, rhs_v, lhs_v, acc_v, send1, recv1, send2, recv2,
    stem_sem, mid_sem, right_sem, gs_send, gs_recv, r_send, r_recv,
):
    cut, y = lax.axis_index("cuts"), lax.axis_index("stem")
    core = lax.rem(cut, NCORE)
    x = lax.rem(cut // NCORE, NX)
    z = cut // (NCORE * NX)
    plane = NX * NCORE * ny
    part = y * NCORE + core
    parts = NCORE * ny
    per = nz // parts
    place = x * parts + part

    def at(z_, x_, part_):
        return ((z_ * NX + x_) * NCORE + lax.rem(part_, NCORE), part_ // NCORE)

    barrier = pltpu.get_barrier_semaphore()

    @pl.loop(1, plane)
    def _(d):
        peer = lax.rem(place + d, plane)
        pl.semaphore_signal(
            barrier, inc=1, device_id=at(z, peer // parts, lax.rem(peer, parts)), device_id_type=MESH
        )

    owner = z // per
    in_own = owner == part

    @pl.loop(0, nz)
    def _(d):
        z_ = lax.rem(z + d, nz)

        @pl.when(jnp.logical_not(jnp.logical_and(d == 0, in_own)))
        def _():
            pl.semaphore_signal(barrier, inc=1, device_id=at(z_, x, owner), device_id_type=MESH)

    blocks = stem_hbm.shape[0]
    copies = [pltpu.make_async_copy(mid_hbm, mid_v, mid_sem)]
    copies.append(pltpu.make_async_copy(stem_hbm, stem_v.at[pl.ds(y * blocks, blocks)], stem_sem))
    copies.append(pltpu.make_async_copy(right_hbm, right_v, right_sem))
    for copy in copies:
        copy.start()

    pl.semaphore_wait(barrier, plane - 1 + per * parts - in_own.astype(jnp.int32))

    rows = stem_hbm.shape[1]
    half = rows // 2
    up, down = lax.rem(y + 1, ny), lax.rem(y + ny - 1, ny)
    far = lax.rem(y + 2, ny)
    other = cut + 1 - 2 * core

    def piece(y_, h):
        return stem_v.at[y_ * blocks + core, pl.ds(h * half, half)]

    def push(n, src, dst, device):
        return pltpu.make_async_remote_copy(
            src_ref=src, dst_ref=dst, send_sem=gs_send.at[n], recv_sem=gs_recv.at[n],
            device_id=device, device_id_type=MESH,
        )

    mine = [stem_hbm.at[core, pl.ds(h * half, half)] for h in (0, 1)]
    first = [
        push(0, mine[0], piece(y, 0), (cut, up)),
        push(1, mine[1], piece(y, 1), (cut, down)),
        push(2, mine[1], piece(y, 1), (cut, up)),
        push(3, mine[0], piece(y, 0), (cut, down)),
    ]
    for copy in first:
        copy.start()
    arrives = [(down, 0), (up, 1), (down, 1), (up, 0), (far, 0), (far, 1)]
    onward = [push(4, piece(down, 0), piece(down, 0), (cut, up)), push(5, piece(up, 1), piece(up, 1), (cut, down))]
    shared = [push(6 + n, piece(*arrives[n]), piece(*arrives[n]), (other, y)) for n in range(6)]

    copies[0].wait()
    depth, width = mid_hbm.shape[1:]
    r = width // 2
    for p in range(mid_hbm.shape[0] // 2):
        a, b = mid_v[2 * p], mid_v[2 * p + 1]
        rhs_v[0:depth, p * width:(p + 1) * width] = jnp.concatenate([a[:, :r], b[:, :r]], axis=1)
        rhs_v[depth:, p * width:(p + 1) * width] = jnp.concatenate([a[:, r:], b[:, r:]], axis=1)

    acc_v[...] = jnp.zeros_like(acc_v)
    tile = 256

    def contract(y_):
        for b in range(blocks):
            s = stem_v[y_ * blocks + b]
            re, im = s[:, :depth], s[:, depth:]
            base = b * 2 * rows
            lhs_v[base:base + rows, :depth] = re
            lhs_v[base:base + rows, depth:] = -im
            lhs_v[base + rows:base + 2 * rows, :depth] = im
            lhs_v[base + rows:base + 2 * rows, depth:] = re
        for n in range(rhs_v.shape[1] // tile):
            f = jnp.dot(
                lhs_v[...], rhs_v[:, n * tile:(n + 1) * tile], preferred_element_type=jnp.float32
            ).astype(jnp.bfloat16)
            for b in range(blocks):
                acc_v[...] += jnp.dot(
                    f[b * 2 * rows:(b + 1) * 2 * rows],
                    right_v[y_ * blocks + b, n * tile:(n + 1) * tile, :],
                    preferred_element_type=jnp.float32,
                )

    copies[1].wait()
    copies[2].wait()
    contract(y)
    for n in (0, 1):
        first[n].wait_recv()
        onward[n].start()
        shared[n].start()
    for n in (2, 3):
        first[n].wait_recv()
        shared[n].start()
    for n in (0, 2):
        shared[n].wait_recv()
    contract(down)
    for n in (0, 1):
        onward[n].wait_recv()
        shared[4 + n].start()
    for n in (1, 3):
        shared[n].wait_recv()
    contract(up)
    for n in (4, 5):
        shared[n].wait_recv()
    contract(far)

    top, bottom = acc_v[0:rows], acc_v[rows:]
    turned = pltpu.roll(bottom, r, axis=1)
    lane = lax.broadcasted_iota(jnp.int32, turned.shape, 1)
    total = top + jnp.where(lane < r, -turned, turned)
    for part_ in range(parts):
        for x_ in range(NX):
            for k in range(per):
                row = (part_ * per + k) * NX + x_
                send1[part_ * NX + x_, k:k + 1, :] = total[row:row + 1]

    @pl.loop(1, plane)
    def _(d):
        peer = lax.rem(place + d, plane)
        x_, part_ = peer // parts, lax.rem(peer, parts)
        pltpu.make_async_remote_copy(
            src_ref=send1.at[part_ * NX + x_], dst_ref=recv1.at[place],
            send_sem=r_send.at[0], recv_sem=r_recv.at[0],
            device_id=at(z, x_, part_), device_id_type=MESH,
        ).start()

    recv1[place] = send1[part * NX + x]
    all1 = pltpu.make_async_remote_copy(
        src_ref=send1.at[pl.ds(0, plane - 1)], dst_ref=recv1.at[pl.ds(0, plane - 1)],
        send_sem=r_send.at[0], recv_sem=r_recv.at[0], device_id=(cut, y), device_id_type=MESH,
    )
    all1.wait_recv()
    sums = recv1[0]
    for n in range(1, plane):
        sums = sums + recv1[n]
    for k in range(per):
        send2[k] = sums[k:k + 1]

    def target(t):
        k, part_ = t // parts, lax.rem(lax.rem(t, parts) + part, parts)
        z_ = part * per + k
        return k, z_, part_

    @pl.loop(0, per * parts)
    def _(t):
        k, z_, part_ = target(t)
        own = jnp.logical_and(z_ == z, part_ == part)

        @pl.when(jnp.logical_not(own))
        def _():
            pltpu.make_async_remote_copy(
                src_ref=send2.at[k], dst_ref=recv2.at[z],
                send_sem=r_send.at[1], recv_sem=r_recv.at[1],
                device_id=at(z_, x, part_), device_id_type=MESH,
            ).start()

        @pl.when(own)
        def _():
            recv2[z] = send2[k]

    def all2(n):
        return pltpu.make_async_remote_copy(
            src_ref=recv2.at[pl.ds(0, n)], dst_ref=recv2.at[pl.ds(0, n)],
            send_sem=r_send.at[1], recv_sem=r_recv.at[1], device_id=(cut, y), device_id_type=MESH,
        )

    @pl.when(in_own)
    def _():
        all2(nz - 1).wait_recv()

    @pl.when(jnp.logical_not(in_own))
    def _():
        all2(nz).wait_recv()

    result = recv2[0]
    for n in range(1, nz):
        result = result + recv2[n]
    out_ref[...] = jnp.where(core == 0, result[:, :r], result[:, r:])

    for copy in first + onward + shared:
        copy.wait_send()
    all1.wait_send()

    @pl.when(in_own)
    def _():
        all2(nz - 1).wait_send()

    @pl.when(jnp.logical_not(in_own))
    def _():
        all2(nz).wait_send()


def on_device(nz, ny, stem_tensor, mid_tensors, right_tensors):
    blocks, rows, width = stem_tensor.shape
    terms, pairs, r, cols = right_tensors.shape
    depth = mid_tensors.shape[1]
    plane = NX * NCORE * ny
    per = nz // (NCORE * ny)
    anywhere = pl.BlockSpec(memory_space=pl.ANY)
    out = pl.pallas_call(
        functools.partial(kernel, nz, ny),
        out_shape=jax.ShapeDtypeStruct((1, cols // 2), jnp.float32),
        in_specs=[anywhere] * 3,
        out_specs=pl.BlockSpec(memory_space=pltpu.VMEM),
        scratch_shapes=[
            pltpu.VMEM((terms, rows, width), jnp.bfloat16),
            pltpu.VMEM(mid_tensors.shape, jnp.bfloat16),
            pltpu.VMEM((terms, pairs * r, cols), jnp.bfloat16),
            pltpu.VMEM((2 * depth, pairs * r), jnp.bfloat16),
            pltpu.VMEM((blocks * 2 * rows, width), jnp.bfloat16),
            pltpu.VMEM((2 * rows, cols), jnp.float32),
            pltpu.VMEM((plane, per, cols), jnp.float32),
            pltpu.VMEM((plane, per, cols), jnp.float32),
            pltpu.VMEM((per, 1, cols), jnp.float32),
            pltpu.VMEM((nz, 1, cols), jnp.float32),
            pltpu.SemaphoreType.DMA,
            pltpu.SemaphoreType.DMA,
            pltpu.SemaphoreType.DMA,
            pltpu.SemaphoreType.DMA((12,)),
            pltpu.SemaphoreType.DMA((12,)),
            pltpu.SemaphoreType.DMA((2,)),
            pltpu.SemaphoreType.DMA((2,)),
        ],
        compiler_params=pltpu.CompilerParams(
            collective_id=0, has_side_effects=True, vmem_limit_bytes=60 * 2**20
        ),
    )(stem_tensor, mid_tensors, right_tensors.reshape(terms, pairs * r, cols))
    return out.reshape(-1)


def solution(mesh):
    return jax.shard_map(
        functools.partial(on_device, mesh.shape["cuts"] // (NX * NCORE), mesh.shape["stem"]),
        mesh=mesh,
        in_specs=(
            P("stem", None, None),
            P(("cuts", "stem"), None, None),
            P(None, ("cuts", "stem"), None, None),
        ),
        out_specs=P("cuts"),
        check_vma=False,
    )
```

```python
import functools

import jax
import jax.numpy as jnp
from jax import lax
from jax.experimental import pallas as pl
from jax.experimental.pallas import tpu as pltpu
from jax.sharding import PartitionSpec as P

MESH = pl.DeviceIdType.MESH
NX = 4
NCORE = 2


def tree_sum(values):
    while len(values) > 1:
        odd = values[len(values) // 2 * 2:]
        values = [a + b for a, b in zip(values[::2], values[1::2])] + odd
    return values[0]


def kernel(
    nz, ny,
    stem_hbm, mid_hbm, right_hbm, out_ref,
    stem_v, mid_v, right_v, rhs_v, lhs_v, mix_v, acc_v, send1, recv1, send2, recv2,
    stem_sem, mid_sem, right_sem, gs_send, gs_recv, r_send, r_recv,
):
    cut, y = lax.axis_index("cuts"), lax.axis_index("stem")
    core = lax.rem(cut, NCORE)
    x = lax.rem(lax.div(cut, NCORE), NX)
    z = lax.div(cut, NCORE * NX)
    plane = NX * NCORE * ny
    parts = NCORE * ny
    part = y * NCORE + core
    per = nz // parts
    xs = [lax.rem(x + d, NX) for d in range(NX)]
    ys = [lax.rem(y + d, ny) for d in range(ny)]
    cores = [core, 1 - core]

    def hops(d, n):
        return min(d, n - d)

    def signal(device):
        pl.semaphore_signal(barrier, inc=1, device_id=device, device_id_type=MESH)

    def at(z_, x_, core_):
        return (z_ * NX + x_) * NCORE + core_

    barrier = pltpu.get_barrier_semaphore()
    for d in range(1, ny):
        signal((cut, ys[d]))
    for d in range(NX):
        for c in range(NCORE):
            if d or c:
                signal((at(z, xs[d], cores[c]), y))
    for d in range(1, nz):
        signal((at(lax.rem(z + d, nz), x, core), y))

    blocks = stem_hbm.shape[0]
    load_stem = pltpu.make_async_copy(stem_hbm, stem_v.at[pl.ds(y * blocks, blocks)], stem_sem)
    load_mid = pltpu.make_async_copy(mid_hbm, mid_v, mid_sem)
    load_right = pltpu.make_async_copy(right_hbm, right_v, right_sem)
    load_stem.start()
    load_mid.start()
    load_right.start()
    pl.semaphore_wait(barrier, (ny - 1) + (NX * NCORE - 1) + (nz - 1))

    rows = stem_hbm.shape[1]
    half = rows // 2
    up, far, down = ys[1], ys[2], ys[3]
    other = at(z, x, cores[1])

    def piece(y_, h):
        return stem_v.at[y_ * blocks + core, pl.ds(h * half, half)]

    def push(n, src, dst, device):
        return pltpu.make_async_remote_copy(
            src_ref=src, dst_ref=dst, send_sem=gs_send.at[n], recv_sem=gs_recv.at[n],
            device_id=device, device_id_type=MESH,
        )

    mine = [stem_hbm.at[core, pl.ds(h * half, half)] for h in (0, 1)]
    first = [
        push(0, mine[0], piece(y, 0), (cut, up)),
        push(1, mine[1], piece(y, 1), (cut, down)),
        push(2, mine[1], piece(y, 1), (cut, up)),
        push(3, mine[0], piece(y, 0), (cut, down)),
    ]
    for copy in first:
        copy.start()
    arrives = [(down, 0), (up, 1), (down, 1), (up, 0), (far, 0), (far, 1)]
    onward = [push(4, piece(down, 0), piece(down, 0), (cut, up)), push(5, piece(up, 1), piece(up, 1), (cut, down))]
    shared = [push(6 + n, piece(*arrives[n]), piece(*arrives[n]), (other, y)) for n in range(6)]

    depth, width = mid_hbm.shape[1:]
    r = width // 2
    load_mid.wait()
    for p in range(mid_hbm.shape[0] // 2):
        a, b = mid_v[2 * p], mid_v[2 * p + 1]
        rhs_v[0:depth, p * width:(p + 1) * width] = jnp.concatenate([a[:, :r], b[:, :r]], axis=1)
        rhs_v[depth:, p * width:(p + 1) * width] = jnp.concatenate([a[:, r:], b[:, r:]], axis=1)

    tile = 256

    def contract(slot, y_, core_, start=False):
        s = stem_v[y_ * blocks + core_]
        re, im = s[:, :depth], s[:, depth:]
        lhs_v[slot, :rows, :depth] = re
        lhs_v[slot, :rows, depth:] = -im
        lhs_v[slot, rows:, :depth] = im
        lhs_v[slot, rows:, depth:] = re
        for n in range(rhs_v.shape[1] // tile):
            mix_v[slot, :, n * tile:(n + 1) * tile] = jnp.dot(
                lhs_v[slot], rhs_v[:, n * tile:(n + 1) * tile], preferred_element_type=jnp.float32
            ).astype(jnp.bfloat16)
        update = jnp.dot(mix_v[slot], right_v[y_ * blocks + core_], preferred_element_type=jnp.float32)
        acc_v[...] = update if start else acc_v[...] + update

    load_stem.wait()
    load_right.wait()
    contract(0, y, cores[0], start=True)
    contract(1, y, cores[1])
    for n in (0, 1):
        first[n].wait_recv()
        onward[n].start()
        shared[n].start()
    for n in (2, 3):
        first[n].wait_recv()
        shared[n].start()
    contract(0, down, cores[0])
    contract(1, up, cores[0])
    for n in (0, 2):
        shared[n].wait_recv()
    for n in (0, 1):
        onward[n].wait_recv()
        shared[4 + n].start()
    contract(0, down, cores[1])
    contract(1, far, cores[0])
    for n in (1, 3):
        shared[n].wait_recv()
    contract(0, up, cores[1])
    for n in (4, 5):
        shared[n].wait_recv()
    contract(1, far, cores[1])

    top, bottom = acc_v[0:rows], acc_v[rows:]
    turned = pltpu.roll(bottom, r, axis=1)
    lane = lax.broadcasted_iota(jnp.int32, turned.shape, 1)
    total = top + jnp.where(lane < r, -turned, turned)
    for part_ in range(parts):
        for x_ in range(NX):
            for k in range(per):
                row = (part_ * per + k) * NX + x_
                send1[part_ * NX + x_, k:k + 1, :] = total[row:row + 1]

    place = x * parts + part
    peers = [(dx, dy, dc) for dx in range(NX) for dy in range(ny) for dc in range(NCORE)]
    peers.sort(key=lambda d: -(hops(d[0], NX) + hops(d[1], ny) + 0.5 * d[2]))
    for dx, dy, dc in peers:
        part_ = ys[dy] * NCORE + cores[dc]
        if dx or dy or dc:
            pltpu.make_async_remote_copy(
                src_ref=send1.at[part_ * NX + xs[dx]], dst_ref=recv1.at[place],
                send_sem=r_send.at[0], recv_sem=r_recv.at[0],
                device_id=(at(z, xs[dx], cores[dc]), ys[dy]), device_id_type=MESH,
            ).start()
    recv1[place] = send1[part * NX + x]
    all1 = pltpu.make_async_remote_copy(
        src_ref=send1.at[pl.ds(0, plane - 1)], dst_ref=recv1.at[pl.ds(0, plane - 1)],
        send_sem=r_send.at[0], recv_sem=r_recv.at[0], device_id=(cut, y), device_id_type=MESH,
    )
    all1.wait_recv()
    sums = tree_sum([recv1[n] for n in range(plane)])
    for k in range(per):
        send2[k] = sums[k:k + 1]

    def deliver(k, device):
        pltpu.make_async_remote_copy(
            src_ref=send2.at[k], dst_ref=recv2.at[z],
            send_sem=r_send.at[1], recv_sem=r_recv.at[1], device_id=device, device_id_type=MESH,
        ).start()

    for dy in sorted(range(ny), key=lambda d: hops(d, ny)):
        for dc in range(NCORE):
            for k in range(per):
                z_ = part * per + k
                device = (at(z_, x, cores[dc]), ys[dy])
                if dy or dc:
                    deliver(k, device)
                else:
                    pl.when(z_ != z)(functools.partial(deliver, k, device))

                    @pl.when(z_ == z)
                    def _():
                        recv2[z] = send2[k]

    in_own = lax.div(z, per) == part

    def all2(n):
        return pltpu.make_async_remote_copy(
            src_ref=recv2.at[pl.ds(0, n)], dst_ref=recv2.at[pl.ds(0, n)],
            send_sem=r_send.at[1], recv_sem=r_recv.at[1], device_id=(cut, y), device_id_type=MESH,
        )

    @pl.when(in_own)
    def _():
        all2(nz - 1).wait_recv()

    @pl.when(jnp.logical_not(in_own))
    def _():
        all2(nz).wait_recv()

    out_ref[...] = tree_sum([recv2[n] for n in range(nz)])

    for copy in first + onward + shared:
        copy.wait_send()
    all1.wait_send()

    @pl.when(in_own)
    def _():
        all2(nz - 1).wait_send()

    @pl.when(jnp.logical_not(in_own))
    def _():
        all2(nz).wait_send()


def on_device(nz, ny, stem_tensor, mid_tensors, right_tensors):
    blocks, rows, width = stem_tensor.shape
    terms, pairs, r, cols = right_tensors.shape
    depth = mid_tensors.shape[1]
    plane = NX * NCORE * ny
    per = nz // (NCORE * ny)
    anywhere = pl.BlockSpec(memory_space=pl.ANY)
    out = pl.pallas_call(
        functools.partial(kernel, nz, ny),
        out_shape=jax.ShapeDtypeStruct((1, cols), jnp.float32),
        in_specs=[anywhere] * 3,
        out_specs=pl.BlockSpec(memory_space=pltpu.VMEM),
        scratch_shapes=[
            pltpu.VMEM((terms, rows, width), jnp.bfloat16),
            pltpu.VMEM(mid_tensors.shape, jnp.bfloat16),
            pltpu.VMEM((terms, pairs * r, cols), jnp.bfloat16),
            pltpu.VMEM((2 * depth, pairs * r), jnp.bfloat16),
            pltpu.VMEM((2, 2 * rows, width), jnp.bfloat16),
            pltpu.VMEM((2, 2 * rows, pairs * r), jnp.bfloat16),
            pltpu.VMEM((2 * rows, cols), jnp.float32),
            pltpu.VMEM((plane, per, cols), jnp.float32),
            pltpu.VMEM((plane, per, cols), jnp.float32),
            pltpu.VMEM((per, 1, cols), jnp.float32),
            pltpu.VMEM((nz, 1, cols), jnp.float32),
            pltpu.SemaphoreType.DMA,
            pltpu.SemaphoreType.DMA,
            pltpu.SemaphoreType.DMA,
            pltpu.SemaphoreType.DMA((12,)),
            pltpu.SemaphoreType.DMA((12,)),
            pltpu.SemaphoreType.DMA((2,)),
            pltpu.SemaphoreType.DMA((2,)),
        ],
        compiler_params=pltpu.CompilerParams(
            collective_id=0, has_side_effects=True, vmem_limit_bytes=60 * 2**20
        ),
    )(stem_tensor, mid_tensors, right_tensors.reshape(terms, pairs * r, cols))
    portion = cols // NCORE
    start = lax.rem(lax.axis_index("cuts"), NCORE) * portion
    return lax.dynamic_slice_in_dim(out.reshape(-1), start, portion)


def solution(mesh):
    return jax.shard_map(
        functools.partial(on_device, mesh.shape["cuts"] // (NX * NCORE), mesh.shape["stem"]),
        mesh=mesh,
        in_specs=(
            P("stem", None, None),
            P(("cuts", "stem"), None, None),
            P(None, ("cuts", "stem"), None, None),
        ),
        out_specs=P("cuts"),
        check_vma=False,
    )
```

```python
import functools

import jax
import jax.numpy as jnp
from jax import lax
from jax.experimental import pallas as pl
from jax.experimental.pallas import tpu as pltpu
from jax.sharding import PartitionSpec as P

MESH = pl.DeviceIdType.MESH
NX = 4
NCORE = 2


def tree_sum(values):
    while len(values) > 1:
        odd = values[len(values) // 2 * 2:]
        values = [a + b for a, b in zip(values[::2], values[1::2])] + odd
    return values[0]


def kernel(
    nz, ny,
    stem_hbm, mid_hbm, right_hbm, out_ref,
    stem_v, mid_v, right_v, rhs_v, lhs_v, mix_v, acc_v, send1, recv1, send2, recv2,
    stem_sem, mid_sem, right_sem, gs_send, gs_recv, r_send, r_recv,
):
    cut, y = lax.axis_index("cuts"), lax.axis_index("stem")
    core = lax.rem(cut, NCORE)
    x = lax.rem(lax.div(cut, NCORE), NX)
    z = lax.div(cut, NCORE * NX)
    plane = NX * NCORE * ny
    parts = NCORE * ny
    part = y * NCORE + core
    per = nz // parts
    xs = [lax.rem(x + d, NX) for d in range(NX)]
    ys = [lax.rem(y + d, ny) for d in range(ny)]
    cores = [core, 1 - core]

    def hops(d, n):
        return min(d, n - d)

    def signal(device):
        pl.semaphore_signal(barrier, inc=1, device_id=device, device_id_type=MESH)

    def at(z_, x_, core_):
        return (z_ * NX + x_) * NCORE + core_

    barrier = pltpu.get_barrier_semaphore()
    for d in range(1, ny):
        signal((cut, ys[d]))
    for d in range(NX):
        for c in range(NCORE):
            if d or c:
                signal((at(z, xs[d], cores[c]), y))
    for d in range(1, nz):
        signal((at(lax.rem(z + d, nz), x, core), y))

    blocks = stem_hbm.shape[0]
    load_stem = pltpu.make_async_copy(stem_hbm, stem_v.at[pl.ds(y * blocks, blocks)], stem_sem)
    load_mid = pltpu.make_async_copy(mid_hbm, mid_v, mid_sem)
    load_right = pltpu.make_async_copy(right_hbm, right_v, right_sem)
    load_stem.start()
    load_mid.start()
    load_right.start()
    pl.semaphore_wait(barrier, (ny - 1) + (NX * NCORE - 1) + (nz - 1))

    rows = stem_hbm.shape[1]
    half = rows // 2
    up, far, down = ys[1], ys[2], ys[3]
    other = at(z, x, cores[1])

    def piece(y_, h):
        return stem_v.at[y_ * blocks + core, pl.ds(h * half, half)]

    def push(n, src, dst, device):
        return pltpu.make_async_remote_copy(
            src_ref=src, dst_ref=dst, send_sem=gs_send.at[n], recv_sem=gs_recv.at[n],
            device_id=device, device_id_type=MESH,
        )

    mine = [stem_hbm.at[core, pl.ds(h * half, half)] for h in (0, 1)]
    arriving = [
        push(0, mine[0], piece(y, 0), (cut, up)),
        push(1, mine[1], piece(y, 1), (cut, down)),
        push(2, mine[1], piece(y, 1), (cut, up)),
        push(3, mine[0], piece(y, 0), (cut, down)),
        push(4, mine[0], piece(y, 0), (cut, far)),
        push(5, mine[1], piece(y, 1), (cut, far)),
    ]
    for copy in arriving:
        copy.start()
    arrived = [piece(down, 0), piece(up, 1), piece(down, 1), piece(up, 0), piece(far, 0), piece(far, 1)]
    shared = [push(6 + n, arrived[n], arrived[n], (other, y)) for n in range(6)]

    def share(*which):
        for n in which:
            arriving[n].wait_recv()
            shared[n].start()

    depth, width = mid_hbm.shape[1:]
    r = width // 2
    load_mid.wait()
    for p in range(mid_hbm.shape[0] // 2):
        a, b = mid_v[2 * p], mid_v[2 * p + 1]
        rhs_v[0:depth, p * width:(p + 1) * width] = jnp.concatenate([a[:, :r], b[:, :r]], axis=1)
        rhs_v[depth:, p * width:(p + 1) * width] = jnp.concatenate([a[:, r:], b[:, r:]], axis=1)

    tile = 256

    def contract(slot, y_, core_, start=False):
        s = stem_v[y_ * blocks + core_]
        re, im = s[:, :depth], s[:, depth:]
        lhs_v[slot, :rows, :depth] = re
        lhs_v[slot, :rows, depth:] = -im
        lhs_v[slot, rows:, :depth] = im
        lhs_v[slot, rows:, depth:] = re
        for n in range(rhs_v.shape[1] // tile):
            mix_v[slot, :, n * tile:(n + 1) * tile] = jnp.dot(
                lhs_v[slot], rhs_v[:, n * tile:(n + 1) * tile], preferred_element_type=jnp.float32
            ).astype(jnp.bfloat16)
        update = jnp.dot(mix_v[slot], right_v[y_ * blocks + core_], preferred_element_type=jnp.float32)
        acc_v[...] = update if start else acc_v[...] + update

    load_stem.wait()
    load_right.wait()
    contract(0, y, cores[0], start=True)
    contract(1, y, cores[1])
    share(0, 1, 2, 3)
    contract(0, down, cores[0])
    contract(1, up, cores[0])
    for n in (0, 2):
        shared[n].wait_recv()
    contract(0, down, cores[1])
    share(4, 5)
    contract(1, far, cores[0])
    for n in (1, 3):
        shared[n].wait_recv()
    contract(0, up, cores[1])
    for n in (4, 5):
        shared[n].wait_recv()
    contract(1, far, cores[1])

    top, bottom = acc_v[0:rows], acc_v[rows:]
    turned = pltpu.roll(bottom, r, axis=1)
    lane = lax.broadcasted_iota(jnp.int32, turned.shape, 1)
    total = top + jnp.where(lane < r, -turned, turned)
    for part_ in range(parts):
        for x_ in range(NX):
            for k in range(per):
                row = (part_ * per + k) * NX + x_
                send1[part_ * NX + x_, k:k + 1, :] = total[row:row + 1]

    place = x * parts + part

    def send(part_, x_):
        pltpu.make_async_remote_copy(
            src_ref=send1.at[part_ * NX + x_], dst_ref=recv1.at[place],
            send_sem=r_send.at[0], recv_sem=r_recv.at[0],
            device_id=(at(z, x_, part_ % NCORE), part_ // NCORE), device_id_type=MESH,
        ).start()

    for part_ in range(parts):
        for x_ in range(NX):
            pl.when(place != x_ * parts + part_)(functools.partial(send, part_, x_))
    recv1[place] = send1[part * NX + x]
    all1 = pltpu.make_async_remote_copy(
        src_ref=send1.at[pl.ds(0, plane - 1)], dst_ref=recv1.at[pl.ds(0, plane - 1)],
        send_sem=r_send.at[0], recv_sem=r_recv.at[0], device_id=(cut, y), device_id_type=MESH,
    )
    all1.wait_recv()
    sums = tree_sum([recv1[n] for n in range(plane)])
    for k in range(per):
        send2[k] = sums[k:k + 1]

    def deliver(k, device):
        pltpu.make_async_remote_copy(
            src_ref=send2.at[k], dst_ref=recv2.at[z],
            send_sem=r_send.at[1], recv_sem=r_recv.at[1], device_id=device, device_id_type=MESH,
        ).start()

    for k in range(per):
        for dy in sorted(range(ny), key=lambda d: hops(d, ny)):
            for dc in reversed(range(NCORE)):
                z_ = part * per + k
                device = (at(z_, x, cores[dc]), ys[dy])
                if dy or dc:
                    deliver(k, device)
                else:
                    pl.when(z_ != z)(functools.partial(deliver, k, device))

                    @pl.when(z_ == z)
                    def _():
                        recv2[z] = send2[k]

    in_own = lax.div(z, per) == part

    def all2(n):
        return pltpu.make_async_remote_copy(
            src_ref=recv2.at[pl.ds(0, n)], dst_ref=recv2.at[pl.ds(0, n)],
            send_sem=r_send.at[1], recv_sem=r_recv.at[1], device_id=(cut, y), device_id_type=MESH,
        )

    @pl.when(in_own)
    def _():
        all2(nz - 1).wait_recv()

    @pl.when(jnp.logical_not(in_own))
    def _():
        all2(nz).wait_recv()

    out_ref[...] = tree_sum([recv2[n] for n in range(nz)])

    for copy in arriving + shared:
        copy.wait_send()
    all1.wait_send()

    @pl.when(in_own)
    def _():
        all2(nz - 1).wait_send()

    @pl.when(jnp.logical_not(in_own))
    def _():
        all2(nz).wait_send()


def on_device(nz, ny, stem_tensor, mid_tensors, right_tensors):
    blocks, rows, width = stem_tensor.shape
    terms, pairs, r, cols = right_tensors.shape
    depth = mid_tensors.shape[1]
    plane = NX * NCORE * ny
    per = nz // (NCORE * ny)
    anywhere = pl.BlockSpec(memory_space=pl.ANY)
    out = pl.pallas_call(
        functools.partial(kernel, nz, ny),
        out_shape=pltpu.VMEM((1, cols), jnp.float32),
        in_specs=[anywhere] * 3,
        out_specs=pl.BlockSpec(memory_space=pltpu.VMEM),
        scratch_shapes=[
            pltpu.VMEM((terms, rows, width), jnp.bfloat16),
            pltpu.VMEM(mid_tensors.shape, jnp.bfloat16),
            pltpu.VMEM((terms, pairs * r, cols), jnp.bfloat16),
            pltpu.VMEM((2 * depth, pairs * r), jnp.bfloat16),
            pltpu.VMEM((2, 2 * rows, width), jnp.bfloat16),
            pltpu.VMEM((2, 2 * rows, pairs * r), jnp.bfloat16),
            pltpu.VMEM((2 * rows, cols), jnp.float32),
            pltpu.VMEM((plane, per, cols), jnp.float32),
            pltpu.VMEM((plane, per, cols), jnp.float32),
            pltpu.VMEM((per, 1, cols), jnp.float32),
            pltpu.VMEM((nz, 1, cols), jnp.float32),
            pltpu.SemaphoreType.DMA,
            pltpu.SemaphoreType.DMA,
            pltpu.SemaphoreType.DMA,
            pltpu.SemaphoreType.DMA((12,)),
            pltpu.SemaphoreType.DMA((12,)),
            pltpu.SemaphoreType.DMA((2,)),
            pltpu.SemaphoreType.DMA((2,)),
        ],
        compiler_params=pltpu.CompilerParams(
            collective_id=0, has_side_effects=True, vmem_limit_bytes=60 * 2**20
        ),
    )(stem_tensor, mid_tensors, right_tensors.reshape(terms, pairs * r, cols))
    portion = cols // NCORE
    start = lax.rem(lax.axis_index("cuts"), NCORE) * portion
    return lax.dynamic_slice_in_dim(out.reshape(-1), start, portion)


def solution(mesh):
    return jax.shard_map(
        functools.partial(on_device, mesh.shape["cuts"] // (NX * NCORE), mesh.shape["stem"]),
        mesh=mesh,
        in_specs=(
            P("stem", None, None),
            P(("cuts", "stem"), None, None),
            P(None, ("cuts", "stem"), None, None),
        ),
        out_specs=P("cuts"),
        check_vma=False,
    )
```

```python
import functools

import jax
import jax.numpy as jnp
from jax import lax
from jax.experimental import pallas as pl
from jax.experimental.pallas import tpu as pltpu
from jax.sharding import PartitionSpec as P

MESH = pl.DeviceIdType.MESH
NX = 4
NCORE = 2


def tree_sum(values):
    while len(values) > 1:
        odd = values[len(values) // 2 * 2:]
        values = [a + b for a, b in zip(values[::2], values[1::2])] + odd
    return values[0]


def kernel(
    nz, ny,
    stem_hbm, mid_hbm, right_hbm, out_ref,
    stem_v, mid_v, right_v, rhs_v, lhs_v, mix_v, acc_v, send1, recv1, send2, recv2,
    stem_sem, mid_sem, right_sem, gs_send, gs_recv, r_send, r_recv, z_sem,
):
    cut, y = lax.axis_index("cuts"), lax.axis_index("stem")
    core = lax.rem(cut, NCORE)
    x = lax.rem(lax.div(cut, NCORE), NX)
    z = lax.div(cut, NCORE * NX)
    plane = NX * NCORE * ny
    parts = NCORE * ny
    part = y * NCORE + core
    per = nz // parts
    xs = [lax.rem(x + d, NX) for d in range(NX)]
    ys = [lax.rem(y + d, ny) for d in range(ny)]
    cores = [core, 1 - core]

    def hops(d, n):
        return min(d, n - d)

    def signal(device):
        pl.semaphore_signal(barrier, inc=1, device_id=device, device_id_type=MESH)

    def at(z_, x_, core_):
        return (z_ * NX + x_) * NCORE + core_

    barrier = pltpu.get_barrier_semaphore()
    for d in range(1, ny):
        signal((cut, ys[d]))
    for d in range(NX):
        for c in range(NCORE):
            if d or c:
                signal((at(z, xs[d], cores[c]), y))
    for d in (1, nz - 1):
        signal((at(lax.rem(z + d, nz), x, core), y))

    blocks = stem_hbm.shape[0]
    load_stem = pltpu.make_async_copy(stem_hbm, stem_v.at[pl.ds(y * blocks, blocks)], stem_sem)
    load_mid = pltpu.make_async_copy(mid_hbm, mid_v, mid_sem)
    load_right = pltpu.make_async_copy(right_hbm, right_v, right_sem)
    load_stem.start()
    load_mid.start()
    load_right.start()
    pl.semaphore_wait(barrier, (ny - 1) + (NX * NCORE - 1) + 2)

    rows = stem_hbm.shape[1]
    half = rows // 2
    up, far, down = ys[1], ys[2], ys[3]
    other = at(z, x, cores[1])

    def piece(y_, h):
        return stem_v.at[y_ * blocks + core, pl.ds(h * half, half)]

    def push(n, src, dst, device):
        return pltpu.make_async_remote_copy(
            src_ref=src, dst_ref=dst, send_sem=gs_send.at[n], recv_sem=gs_recv.at[n],
            device_id=device, device_id_type=MESH,
        )

    mine = [stem_hbm.at[core, pl.ds(h * half, half)] for h in (0, 1)]
    arriving = [
        push(0, mine[0], piece(y, 0), (cut, up)),
        push(1, mine[1], piece(y, 1), (cut, down)),
        push(2, mine[1], piece(y, 1), (cut, up)),
        push(3, mine[0], piece(y, 0), (cut, down)),
        push(4, mine[0], piece(y, 0), (cut, far)),
        push(5, mine[1], piece(y, 1), (cut, far)),
    ]
    for copy in arriving:
        copy.start()

    rounds, reach = [], 1
    while reach < nz // 2:
        rounds.append((2 * len(rounds), reach))
        reach += rounds[-1][1]

    def announce(n):
        at_sem, step = rounds[n]
        for way, d in enumerate((step, nz - step)):
            device = (at(lax.rem(z + d, nz), x, core), y)
            pl.semaphore_signal(z_sem.at[at_sem + way], inc=1, device_id=device, device_id_type=MESH)

    def heard(n):
        for way in range(2):
            pl.semaphore_wait(z_sem.at[rounds[n][0] + way], 1)

    announce(0)
    arrived = [piece(down, 0), piece(up, 1), piece(down, 1), piece(up, 0), piece(far, 0), piece(far, 1)]
    shared = [push(6 + n, arrived[n], arrived[n], (other, y)) for n in range(6)]

    def share(*which):
        for n in which:
            arriving[n].wait_recv()
            shared[n].start()

    depth, width = mid_hbm.shape[1:]
    r = width // 2
    load_mid.wait()
    for p in range(mid_hbm.shape[0] // 2):
        a, b = mid_v[2 * p], mid_v[2 * p + 1]
        rhs_v[0:depth, p * width:(p + 1) * width] = jnp.concatenate([a[:, :r], b[:, :r]], axis=1)
        rhs_v[depth:, p * width:(p + 1) * width] = jnp.concatenate([a[:, r:], b[:, r:]], axis=1)

    tile = 256

    def contract(slot, y_, core_, start=False):
        s = stem_v[y_ * blocks + core_]
        re, im = s[:, :depth], s[:, depth:]
        lhs_v[slot, :rows, :depth] = re
        lhs_v[slot, :rows, depth:] = -im
        lhs_v[slot, rows:, :depth] = im
        lhs_v[slot, rows:, depth:] = re
        for n in range(rhs_v.shape[1] // tile):
            mix_v[slot, :, n * tile:(n + 1) * tile] = jnp.dot(
                lhs_v[slot], rhs_v[:, n * tile:(n + 1) * tile], preferred_element_type=jnp.float32
            ).astype(jnp.bfloat16)
        update = jnp.dot(mix_v[slot], right_v[y_ * blocks + core_], preferred_element_type=jnp.float32)
        acc_v[...] = update if start else acc_v[...] + update

    load_stem.wait()
    load_right.wait()
    heard(0)
    announce(1)
    contract(0, y, cores[0], start=True)
    contract(1, y, cores[1])
    share(0, 1, 2, 3)
    heard(1)
    announce(2)
    contract(0, down, cores[0])
    contract(1, up, cores[0])
    for n in (0, 2):
        shared[n].wait_recv()
    contract(0, down, cores[1])
    share(4, 5)
    contract(1, far, cores[0])
    for n in (1, 3):
        shared[n].wait_recv()
    contract(0, up, cores[1])
    for n in (4, 5):
        shared[n].wait_recv()
    contract(1, far, cores[1])

    heard(2)
    top, bottom = acc_v[0:rows], acc_v[rows:]
    turned = pltpu.roll(bottom, r, axis=1)
    lane = lax.broadcasted_iota(jnp.int32, turned.shape, 1)
    total = top + jnp.where(lane < r, -turned, turned)
    for part_ in range(parts):
        for x_ in range(NX):
            for k in range(per):
                row = (part_ * per + k) * NX + x_
                send1[part_ * NX + x_, k:k + 1, :] = total[row:row + 1]

    place = x * parts + part

    def send(part_, x_):
        pltpu.make_async_remote_copy(
            src_ref=send1.at[part_ * NX + x_], dst_ref=recv1.at[place],
            send_sem=r_send.at[0], recv_sem=r_recv.at[0],
            device_id=(at(z, x_, part_ % NCORE), part_ // NCORE), device_id_type=MESH,
        ).start()

    for part_ in range(parts):
        for x_ in range(NX):
            pl.when(place != x_ * parts + part_)(functools.partial(send, part_, x_))
    recv1[place] = send1[part * NX + x]
    all1 = pltpu.make_async_remote_copy(
        src_ref=send1.at[pl.ds(0, plane - 1)], dst_ref=recv1.at[pl.ds(0, plane - 1)],
        send_sem=r_send.at[0], recv_sem=r_recv.at[0], device_id=(cut, y), device_id_type=MESH,
    )
    all1.wait_recv()
    sums = tree_sum([recv1[n] for n in range(plane)])
    for k in range(per):
        send2[k] = sums[k:k + 1]

    def deliver(k, device):
        pltpu.make_async_remote_copy(
            src_ref=send2.at[k], dst_ref=recv2.at[z],
            send_sem=r_send.at[1], recv_sem=r_recv.at[1], device_id=device, device_id_type=MESH,
        ).start()

    for k in range(per):
        for dy in sorted(range(ny), key=lambda d: hops(d, ny)):
            for dc in reversed(range(NCORE)):
                z_ = part * per + k
                device = (at(z_, x, cores[dc]), ys[dy])
                if dy or dc:
                    deliver(k, device)
                else:
                    pl.when(z_ != z)(functools.partial(deliver, k, device))

                    @pl.when(z_ == z)
                    def _():
                        recv2[z] = send2[k]

    in_own = lax.div(z, per) == part

    def all2(n):
        return pltpu.make_async_remote_copy(
            src_ref=recv2.at[pl.ds(0, n)], dst_ref=recv2.at[pl.ds(0, n)],
            send_sem=r_send.at[1], recv_sem=r_recv.at[1], device_id=(cut, y), device_id_type=MESH,
        )

    @pl.when(in_own)
    def _():
        all2(nz - 1).wait_recv()

    @pl.when(jnp.logical_not(in_own))
    def _():
        all2(nz).wait_recv()

    out_ref[...] = tree_sum([recv2[n] for n in range(nz)])

    for copy in arriving + shared:
        copy.wait_send()
    all1.wait_send()

    @pl.when(in_own)
    def _():
        all2(nz - 1).wait_send()

    @pl.when(jnp.logical_not(in_own))
    def _():
        all2(nz).wait_send()


def on_device(nz, ny, stem_tensor, mid_tensors, right_tensors):
    blocks, rows, width = stem_tensor.shape
    terms, pairs, r, cols = right_tensors.shape
    depth = mid_tensors.shape[1]
    plane = NX * NCORE * ny
    per = nz // (NCORE * ny)
    anywhere = pl.BlockSpec(memory_space=pl.ANY)
    out = pl.pallas_call(
        functools.partial(kernel, nz, ny),
        out_shape=pltpu.VMEM((1, cols), jnp.float32),
        in_specs=[anywhere] * 3,
        out_specs=pl.BlockSpec(memory_space=pltpu.VMEM),
        scratch_shapes=[
            pltpu.VMEM((terms, rows, width), jnp.bfloat16),
            pltpu.VMEM(mid_tensors.shape, jnp.bfloat16),
            pltpu.VMEM((terms, pairs * r, cols), jnp.bfloat16),
            pltpu.VMEM((2 * depth, pairs * r), jnp.bfloat16),
            pltpu.VMEM((2, 2 * rows, width), jnp.bfloat16),
            pltpu.VMEM((2, 2 * rows, pairs * r), jnp.bfloat16),
            pltpu.VMEM((2 * rows, cols), jnp.float32),
            pltpu.VMEM((plane, per, cols), jnp.float32),
            pltpu.VMEM((plane, per, cols), jnp.float32),
            pltpu.VMEM((per, 1, cols), jnp.float32),
            pltpu.VMEM((nz, 1, cols), jnp.float32),
            pltpu.SemaphoreType.DMA,
            pltpu.SemaphoreType.DMA,
            pltpu.SemaphoreType.DMA,
            pltpu.SemaphoreType.DMA((12,)),
            pltpu.SemaphoreType.DMA((12,)),
            pltpu.SemaphoreType.DMA((2,)),
            pltpu.SemaphoreType.DMA((2,)),
            pltpu.SemaphoreType.REGULAR((2 * nz.bit_length(),)),
        ],
        compiler_params=pltpu.CompilerParams(
            collective_id=0, has_side_effects=True, vmem_limit_bytes=60 * 2**20
        ),
    )(stem_tensor, mid_tensors, right_tensors.reshape(terms, pairs * r, cols))
    portion = cols // NCORE
    start = lax.rem(lax.axis_index("cuts"), NCORE) * portion
    return lax.dynamic_slice_in_dim(out.reshape(-1), start, portion)


def solution(mesh):
    return jax.shard_map(
        functools.partial(on_device, mesh.shape["cuts"] // (NX * NCORE), mesh.shape["stem"]),
        mesh=mesh,
        in_specs=(
            P("stem", None, None),
            P(("cuts", "stem"), None, None),
            P(None, ("cuts", "stem"), None, None),
        ),
        out_specs=P("cuts"),
        check_vma=False,
    )
```

```python
import functools

import jax
import jax.numpy as jnp
from jax import lax
from jax.experimental import pallas as pl
from jax.experimental.pallas import tpu as pltpu
from jax.sharding import PartitionSpec as P

MESH = pl.DeviceIdType.MESH
NX = 4
NCORE = 2


def tree_sum(values):
    while len(values) > 1:
        odd = values[len(values) // 2 * 2:]
        values = [a + b for a, b in zip(values[::2], values[1::2])] + odd
    return values[0]


def kernel(
    nz, ny,
    stem_hbm, mid_hbm, right_hbm, out_ref,
    stem_v, mid_v, right_v, rhs_v, lhs_v, mix_v, acc_v, send1, recv1, send2, recv2,
    stem_sem, mid_sem, right_sem, gs_send, gs_recv, r_send, r_recv, z_sem,
):
    cut, y = lax.axis_index("cuts"), lax.axis_index("stem")
    core = lax.rem(cut, NCORE)
    x = lax.rem(lax.div(cut, NCORE), NX)
    z = lax.div(cut, NCORE * NX)
    plane = NX * NCORE * ny
    parts = NCORE * ny
    part = y * NCORE + core
    per = nz // parts
    xs = [lax.rem(x + d, NX) for d in range(NX)]
    ys = [lax.rem(y + d, ny) for d in range(ny)]
    cores = [core, 1 - core]

    def hops(d, n):
        return min(d, n - d)

    def signal(device):
        pl.semaphore_signal(barrier, inc=1, device_id=device, device_id_type=MESH)

    def at(z_, x_, core_):
        return (z_ * NX + x_) * NCORE + core_

    blocks = stem_hbm.shape[0]
    load_stem = pltpu.make_async_copy(stem_hbm, stem_v.at[pl.ds(y * blocks, blocks)], stem_sem)
    load_stem.start()

    barrier = pltpu.get_barrier_semaphore()
    for d in range(1, ny):
        signal((cut, ys[d]))
    for d in range(NX):
        for c in range(NCORE):
            if d or c:
                signal((at(z, xs[d], cores[c]), y))
    for d in (1, 2, nz - 2, nz - 1):
        signal((at(lax.rem(z + d, nz), x, core), y))

    load_mid = pltpu.make_async_copy(mid_hbm, mid_v, mid_sem)
    load_right = pltpu.make_async_copy(right_hbm, right_v, right_sem)
    load_mid.start()
    load_right.start()
    pl.semaphore_wait(barrier, (ny - 1) + (NX * NCORE - 1) + 4)

    rows = stem_hbm.shape[1]
    half = rows // 2
    up, far, down = ys[1], ys[2], ys[3]
    other = at(z, x, cores[1])

    def piece(y_, h):
        return stem_v.at[y_ * blocks + core, pl.ds(h * half, half)]

    def push(n, src, dst, device):
        return pltpu.make_async_remote_copy(
            src_ref=src, dst_ref=dst, send_sem=gs_send.at[n], recv_sem=gs_recv.at[n],
            device_id=device, device_id_type=MESH,
        )

    load_stem.wait()
    mine = [piece(y, 0), piece(y, 1)]
    arriving = [
        push(0, mine[0], piece(y, 0), (cut, up)),
        push(1, mine[1], piece(y, 1), (cut, down)),
        push(2, mine[1], piece(y, 1), (cut, up)),
        push(3, mine[0], piece(y, 0), (cut, down)),
        push(4, piece(down, 0), piece(down, 0), (cut, up)),
        push(5, piece(up, 1), piece(up, 1), (cut, down)),
    ]
    for copy in arriving[:4]:
        copy.start()

    rounds, reach = [], 2
    while reach < nz // 2:
        rounds.append((2 * len(rounds), reach))
        reach += rounds[-1][1]

    def announce(n):
        at_sem, step = rounds[n]
        for way, d in enumerate((step, nz - step)):
            device = (at(lax.rem(z + d, nz), x, core), y)
            pl.semaphore_signal(z_sem.at[at_sem + way], inc=1, device_id=device, device_id_type=MESH)

    def heard(n):
        for way in range(2):
            pl.semaphore_wait(z_sem.at[rounds[n][0] + way], 1)

    announce(0)
    arrived = [piece(down, 0), piece(up, 1), piece(down, 1), piece(up, 0), piece(far, 0), piece(far, 1)]
    shared = [push(6 + n, arrived[n], arrived[n], (other, y)) for n in range(6)]

    def pass_on(n):
        arriving[n].wait_recv()
        arriving[4 + n].start()

    def share(*which):
        for n in which:
            arriving[n].wait_recv()
            shared[n].start()

    depth, width = mid_hbm.shape[1:]
    r = width // 2
    load_mid.wait()
    for p in range(mid_hbm.shape[0] // 2):
        a, b = mid_v[2 * p], mid_v[2 * p + 1]
        rhs_v[0:depth, p * width:(p + 1) * width] = jnp.concatenate([a[:, :r], b[:, :r]], axis=1)
        rhs_v[depth:, p * width:(p + 1) * width] = jnp.concatenate([a[:, r:], b[:, r:]], axis=1)

    tile = 256

    def contract(slot, y_, core_, start=False):
        s = stem_v[y_ * blocks + core_]
        re, im = s[:, :depth], s[:, depth:]
        lhs_v[slot, :rows, :depth] = re
        lhs_v[slot, :rows, depth:] = -im
        lhs_v[slot, rows:, :depth] = im
        lhs_v[slot, rows:, depth:] = re
        for n in range(rhs_v.shape[1] // tile):
            mix_v[slot, :, n * tile:(n + 1) * tile] = jnp.dot(
                lhs_v[slot], rhs_v[:, n * tile:(n + 1) * tile], preferred_element_type=jnp.float32
            ).astype(jnp.bfloat16)
        update = jnp.dot(mix_v[slot], right_v[y_ * blocks + core_], preferred_element_type=jnp.float32)
        acc_v[...] = update if start else acc_v[...] + update

    load_right.wait()
    contract(0, y, cores[0], start=True)
    heard(0)
    announce(1)
    contract(1, y, cores[1])
    pass_on(0)
    pass_on(1)
    for n in (0, 1):
        shared[n].start()
    share(2, 3)
    contract(0, down, cores[0])
    contract(1, up, cores[0])
    for n in (0, 2):
        shared[n].wait_recv()
    contract(0, down, cores[1])
    for n in (1, 3):
        shared[n].wait_recv()
    contract(1, up, cores[1])
    share(4, 5)
    contract(0, far, cores[0])
    for n in (4, 5):
        shared[n].wait_recv()
    contract(1, far, cores[1])

    heard(1)
    top, bottom = acc_v[0:rows], acc_v[rows:]
    turned = pltpu.roll(bottom, r, axis=1)
    lane = lax.broadcasted_iota(jnp.int32, turned.shape, 1)
    total = top + jnp.where(lane < r, -turned, turned)
    place = x * parts + part

    def send(part_, x_):
        pltpu.make_async_remote_copy(
            src_ref=send1.at[part_ * NX + x_], dst_ref=recv1.at[place],
            send_sem=r_send.at[0], recv_sem=r_recv.at[0],
            device_id=(at(z, x_, part_ % NCORE), part_ // NCORE), device_id_type=MESH,
        ).start()

    for part_ in range(parts):
        for x_ in range(NX):
            for k in range(per):
                row = (part_ * per + k) * NX + x_
                send1[part_ * NX + x_, k:k + 1, :] = total[row:row + 1]
        for x_ in range(NX):
            pl.when(place != x_ * parts + part_)(functools.partial(send, part_, x_))
    recv1[place] = send1[part * NX + x]
    all1 = pltpu.make_async_remote_copy(
        src_ref=send1.at[pl.ds(0, plane - 1)], dst_ref=recv1.at[pl.ds(0, plane - 1)],
        send_sem=r_send.at[0], recv_sem=r_recv.at[0], device_id=(cut, y), device_id_type=MESH,
    )
    all1.wait_recv()
    sums = tree_sum([recv1[n] for n in range(plane)])
    for k in range(per):
        send2[k] = sums[k:k + 1]

    def deliver(k, device):
        pltpu.make_async_remote_copy(
            src_ref=send2.at[k], dst_ref=recv2.at[z],
            send_sem=r_send.at[1], recv_sem=r_recv.at[1], device_id=device, device_id_type=MESH,
        ).start()

    for k in range(per):
        for dy in sorted(range(ny), key=lambda d: hops(d, ny)):
            for dc in reversed(range(NCORE)):
                z_ = part * per + k
                device = (at(z_, x, cores[dc]), ys[dy])
                if dy or dc:
                    deliver(k, device)
                else:
                    pl.when(z_ != z)(functools.partial(deliver, k, device))

                    @pl.when(z_ == z)
                    def _():
                        recv2[z] = send2[k]

    in_own = lax.div(z, per) == part

    def all2(n):
        return pltpu.make_async_remote_copy(
            src_ref=recv2.at[pl.ds(0, n)], dst_ref=recv2.at[pl.ds(0, n)],
            send_sem=r_send.at[1], recv_sem=r_recv.at[1], device_id=(cut, y), device_id_type=MESH,
        )

    @pl.when(in_own)
    def _():
        all2(nz - 1).wait_recv()

    @pl.when(jnp.logical_not(in_own))
    def _():
        all2(nz).wait_recv()

    out_ref[...] = tree_sum([recv2[n] for n in range(nz)])

    for copy in arriving + shared:
        copy.wait_send()
    all1.wait_send()

    @pl.when(in_own)
    def _():
        all2(nz - 1).wait_send()

    @pl.when(jnp.logical_not(in_own))
    def _():
        all2(nz).wait_send()


def on_device(nz, ny, stem_tensor, mid_tensors, right_tensors):
    blocks, rows, width = stem_tensor.shape
    terms, pairs, r, cols = right_tensors.shape
    depth = mid_tensors.shape[1]
    plane = NX * NCORE * ny
    per = nz // (NCORE * ny)
    anywhere = pl.BlockSpec(memory_space=pl.ANY)
    out = pl.pallas_call(
        functools.partial(kernel, nz, ny),
        out_shape=pltpu.VMEM((1, cols), jnp.float32),
        in_specs=[anywhere] * 3,
        out_specs=pl.BlockSpec(memory_space=pltpu.VMEM),
        scratch_shapes=[
            pltpu.VMEM((terms, rows, width), jnp.bfloat16),
            pltpu.VMEM(mid_tensors.shape, jnp.bfloat16),
            pltpu.VMEM((terms, pairs * r, cols), jnp.bfloat16),
            pltpu.VMEM((2 * depth, pairs * r), jnp.bfloat16),
            pltpu.VMEM((2, 2 * rows, width), jnp.bfloat16),
            pltpu.VMEM((2, 2 * rows, pairs * r), jnp.bfloat16),
            pltpu.VMEM((2 * rows, cols), jnp.float32),
            pltpu.VMEM((plane, per, cols), jnp.float32),
            pltpu.VMEM((plane, per, cols), jnp.float32),
            pltpu.VMEM((per, 1, cols), jnp.float32),
            pltpu.VMEM((nz, 1, cols), jnp.float32),
            pltpu.SemaphoreType.DMA,
            pltpu.SemaphoreType.DMA,
            pltpu.SemaphoreType.DMA,
            pltpu.SemaphoreType.DMA((12,)),
            pltpu.SemaphoreType.DMA((12,)),
            pltpu.SemaphoreType.DMA((2,)),
            pltpu.SemaphoreType.DMA((2,)),
            pltpu.SemaphoreType.REGULAR((2 * nz.bit_length(),)),
        ],
        compiler_params=pltpu.CompilerParams(
            collective_id=0, has_side_effects=True, vmem_limit_bytes=60 * 2**20
        ),
    )(stem_tensor, mid_tensors, right_tensors.reshape(terms, pairs * r, cols))
    portion = cols // NCORE
    start = lax.rem(lax.axis_index("cuts"), NCORE) * portion
    return lax.dynamic_slice_in_dim(out.reshape(-1), start, portion)


def solution(mesh):
    return jax.shard_map(
        functools.partial(on_device, mesh.shape["cuts"] // (NX * NCORE), mesh.shape["stem"]),
        mesh=mesh,
        in_specs=(
            P("stem", None, None),
            P(("cuts", "stem"), None, None),
            P(None, ("cuts", "stem"), None, None),
        ),
        out_specs=P("cuts"),
        check_vma=False,
    )
```

```python
import functools

import jax
import jax.numpy as jnp
from jax import lax
from jax.experimental import pallas as pl
from jax.experimental.pallas import tpu as pltpu
from jax.sharding import PartitionSpec as P

MESH = pl.DeviceIdType.MESH
NX = 4
NCORE = 2


def tree_sum(values):
    while len(values) > 1:
        odd = values[len(values) // 2 * 2:]
        values = [a + b for a, b in zip(values[::2], values[1::2])] + odd
    return values[0]


def kernel(
    nz, ny,
    stem_hbm, mid_hbm, right_hbm, out_ref,
    stem_v, mid_v, right_v, rhs_v, lhs_v, mix_v, acc_v, send1, recv1, send2, recv2,
    stem_sem, mid_sem, right_sem, gs_send, gs_recv, r_send, r_recv, round_sem,
):
    cut, y = lax.axis_index("cuts"), lax.axis_index("stem")
    core = lax.rem(cut, NCORE)
    x = lax.rem(lax.div(cut, NCORE), NX)
    z = lax.div(cut, NCORE * NX)
    plane = NX * NCORE * ny
    parts = NCORE * ny
    part = y * NCORE + core
    per = nz // parts
    xs = [lax.rem(x + d, NX) for d in range(NX)]
    ys = [lax.rem(y + d, ny) for d in range(ny)]
    cores = [core, 1 - core]

    def hops(d, n):
        return min(d, n - d)

    def signal(device):
        pl.semaphore_signal(barrier, inc=1, device_id=device, device_id_type=MESH)

    def at(z_, x_, core_):
        return (z_ * NX + x_) * NCORE + core_

    blocks = stem_hbm.shape[0]
    load_stem = pltpu.make_async_copy(stem_hbm, stem_v.at[pl.ds(y * blocks, blocks)], stem_sem)
    load_stem.start()

    barrier = pltpu.get_barrier_semaphore()

    def zs(d):
        return (at(lax.rem(z + d, nz), x, core), y)

    near = [(cut, ys[1]), (cut, ys[ny - 1]), (at(z, x, cores[1]), y)]
    near += [(at(z, xs[d], core), y) for d in (1, NX - 1)] + [zs(d) for d in (1, nz - 1)]
    for device in near:
        signal(device)

    rounds = [
        near,
        [(at(z, xs[2], core), y), (cut, ys[2]), zs(2), zs(nz - 2)],
        [(at(z, x, cores[1]), y), zs(4), zs(nz - 4)],
    ]

    def announce(n):
        for device in rounds[n]:
            pl.semaphore_signal(round_sem.at[n], inc=1, device_id=device, device_id_type=MESH)

    def heard(n):
        pl.semaphore_wait(round_sem.at[n], len(rounds[n]))

    load_mid = pltpu.make_async_copy(mid_hbm, mid_v, mid_sem)
    load_right = pltpu.make_async_copy(right_hbm, right_v, right_sem)
    load_mid.start()
    load_right.start()
    pl.semaphore_wait(barrier, len(near))

    rows = stem_hbm.shape[1]
    half = rows // 2
    up, far, down = ys[1], ys[2], ys[3]
    other = at(z, x, cores[1])

    def piece(y_, h):
        return stem_v.at[y_ * blocks + core, pl.ds(h * half, half)]

    def push(n, src, dst, device):
        return pltpu.make_async_remote_copy(
            src_ref=src, dst_ref=dst, send_sem=gs_send.at[n], recv_sem=gs_recv.at[n],
            device_id=device, device_id_type=MESH,
        )

    load_stem.wait()
    mine = [piece(y, 0), piece(y, 1)]
    arriving = [
        push(0, mine[0], piece(y, 0), (cut, up)),
        push(1, mine[1], piece(y, 1), (cut, down)),
        push(2, mine[1], piece(y, 1), (cut, up)),
        push(3, mine[0], piece(y, 0), (cut, down)),
        push(4, piece(down, 0), piece(down, 0), (cut, up)),
        push(5, piece(up, 1), piece(up, 1), (cut, down)),
    ]
    for copy in arriving[:4]:
        copy.start()

    announce(0)
    arrived = [piece(down, 0), piece(up, 1), piece(down, 1), piece(up, 0), piece(far, 0), piece(far, 1)]
    shared = [push(6 + n, arrived[n], arrived[n], (other, y)) for n in range(6)]

    def pass_on(n):
        arriving[n].wait_recv()
        arriving[4 + n].start()

    def share(*which):
        for n in which:
            arriving[n].wait_recv()
            shared[n].start()

    depth, width = mid_hbm.shape[1:]
    r = width // 2
    load_mid.wait()
    for p in range(mid_hbm.shape[0] // 2):
        a, b = mid_v[2 * p], mid_v[2 * p + 1]
        rhs_v[0:depth, p * width:(p + 1) * width] = jnp.concatenate([a[:, :r], b[:, :r]], axis=1)
        rhs_v[depth:, p * width:(p + 1) * width] = jnp.concatenate([a[:, r:], b[:, r:]], axis=1)

    tile = 256

    def contract(slot, y_, core_, start=False):
        s = stem_v[y_ * blocks + core_]
        re, im = s[:, :depth], s[:, depth:]
        lhs_v[slot, :rows, :depth] = re
        lhs_v[slot, :rows, depth:] = -im
        lhs_v[slot, rows:, :depth] = im
        lhs_v[slot, rows:, depth:] = re
        for n in range(rhs_v.shape[1] // tile):
            mix_v[slot, :, n * tile:(n + 1) * tile] = jnp.dot(
                lhs_v[slot], rhs_v[:, n * tile:(n + 1) * tile], preferred_element_type=jnp.float32
            ).astype(jnp.bfloat16)
        update = jnp.dot(mix_v[slot], right_v[y_ * blocks + core_], preferred_element_type=jnp.float32)
        acc_v[...] = update if start else acc_v[...] + update

    load_right.wait()
    heard(0)
    announce(1)
    contract(0, y, cores[0], start=True)
    contract(1, y, cores[1])
    pass_on(0)
    pass_on(1)
    heard(1)
    announce(2)
    for n in (0, 1):
        shared[n].start()
    share(2, 3)
    contract(0, down, cores[0])
    contract(1, up, cores[0])
    for n in (0, 2):
        shared[n].wait_recv()
    contract(0, down, cores[1])
    for n in (1, 3):
        shared[n].wait_recv()
    contract(1, up, cores[1])
    share(4, 5)
    contract(0, far, cores[0])
    for n in (4, 5):
        shared[n].wait_recv()
    contract(1, far, cores[1])

    heard(2)
    top, bottom = acc_v[0:rows], acc_v[rows:]
    turned = pltpu.roll(bottom, r, axis=1)
    lane = lax.broadcasted_iota(jnp.int32, turned.shape, 1)
    total = top + jnp.where(lane < r, -turned, turned)
    place = x * parts + part

    def send(part_, x_):
        pltpu.make_async_remote_copy(
            src_ref=send1.at[part_ * NX + x_], dst_ref=recv1.at[place],
            send_sem=r_send.at[0], recv_sem=r_recv.at[0],
            device_id=(at(z, x_, part_ % NCORE), part_ // NCORE), device_id_type=MESH,
        ).start()

    for part_ in range(parts):
        for x_ in range(NX):
            for k in range(per):
                row = (part_ * per + k) * NX + x_
                send1[part_ * NX + x_, k:k + 1, :] = total[row:row + 1]
        for x_ in range(NX):
            pl.when(place != x_ * parts + part_)(functools.partial(send, part_, x_))
    recv1[place] = send1[part * NX + x]
    all1 = pltpu.make_async_remote_copy(
        src_ref=send1.at[pl.ds(0, plane - 1)], dst_ref=recv1.at[pl.ds(0, plane - 1)],
        send_sem=r_send.at[0], recv_sem=r_recv.at[0], device_id=(cut, y), device_id_type=MESH,
    )
    all1.wait_recv()
    sums = tree_sum([recv1[n] for n in range(plane)])
    for k in range(per):
        send2[k] = sums[k:k + 1]

    def deliver(k, device):
        pltpu.make_async_remote_copy(
            src_ref=send2.at[k], dst_ref=recv2.at[z],
            send_sem=r_send.at[1], recv_sem=r_recv.at[1], device_id=device, device_id_type=MESH,
        ).start()

    for k in range(per):
        for dy in sorted(range(ny), key=lambda d: hops(d, ny)):
            for dc in reversed(range(NCORE)):
                z_ = part * per + k
                device = (at(z_, x, cores[dc]), ys[dy])
                if dy or dc:
                    deliver(k, device)
                else:
                    pl.when(z_ != z)(functools.partial(deliver, k, device))

                    @pl.when(z_ == z)
                    def _():
                        recv2[z] = send2[k]

    in_own = lax.div(z, per) == part

    def all2(n):
        return pltpu.make_async_remote_copy(
            src_ref=recv2.at[pl.ds(0, n)], dst_ref=recv2.at[pl.ds(0, n)],
            send_sem=r_send.at[1], recv_sem=r_recv.at[1], device_id=(cut, y), device_id_type=MESH,
        )

    @pl.when(in_own)
    def _():
        all2(nz - 1).wait_recv()

    @pl.when(jnp.logical_not(in_own))
    def _():
        all2(nz).wait_recv()

    out_ref[...] = tree_sum([recv2[n] for n in range(nz)])

    for copy in arriving + shared:
        copy.wait_send()
    all1.wait_send()

    @pl.when(in_own)
    def _():
        all2(nz - 1).wait_send()

    @pl.when(jnp.logical_not(in_own))
    def _():
        all2(nz).wait_send()


def on_device(nz, ny, stem_tensor, mid_tensors, right_tensors):
    blocks, rows, width = stem_tensor.shape
    terms, pairs, r, cols = right_tensors.shape
    depth = mid_tensors.shape[1]
    plane = NX * NCORE * ny
    per = nz // (NCORE * ny)
    anywhere = pl.BlockSpec(memory_space=pl.ANY)
    out = pl.pallas_call(
        functools.partial(kernel, nz, ny),
        out_shape=pltpu.VMEM((1, cols), jnp.float32),
        in_specs=[anywhere] * 3,
        out_specs=pl.BlockSpec(memory_space=pltpu.VMEM),
        scratch_shapes=[
            pltpu.VMEM((terms, rows, width), jnp.bfloat16),
            pltpu.VMEM(mid_tensors.shape, jnp.bfloat16),
            pltpu.VMEM((terms, pairs * r, cols), jnp.bfloat16),
            pltpu.VMEM((2 * depth, pairs * r), jnp.bfloat16),
            pltpu.VMEM((2, 2 * rows, width), jnp.bfloat16),
            pltpu.VMEM((2, 2 * rows, pairs * r), jnp.bfloat16),
            pltpu.VMEM((2 * rows, cols), jnp.float32),
            pltpu.VMEM((plane, per, cols), jnp.float32),
            pltpu.VMEM((plane, per, cols), jnp.float32),
            pltpu.VMEM((per, 1, cols), jnp.float32),
            pltpu.VMEM((nz, 1, cols), jnp.float32),
            pltpu.SemaphoreType.DMA,
            pltpu.SemaphoreType.DMA,
            pltpu.SemaphoreType.DMA,
            pltpu.SemaphoreType.DMA((12,)),
            pltpu.SemaphoreType.DMA((12,)),
            pltpu.SemaphoreType.DMA((2,)),
            pltpu.SemaphoreType.DMA((2,)),
            pltpu.SemaphoreType.REGULAR((3,)),
        ],
        compiler_params=pltpu.CompilerParams(
            collective_id=0, has_side_effects=True, vmem_limit_bytes=60 * 2**20
        ),
    )(stem_tensor, mid_tensors, right_tensors.reshape(terms, pairs * r, cols))
    portion = cols // NCORE
    start = lax.rem(lax.axis_index("cuts"), NCORE) * portion
    return lax.dynamic_slice_in_dim(out.reshape(-1), start, portion)


def solution(mesh):
    return jax.shard_map(
        functools.partial(on_device, mesh.shape["cuts"] // (NX * NCORE), mesh.shape["stem"]),
        mesh=mesh,
        in_specs=(
            P("stem", None, None),
            P(("cuts", "stem"), None, None),
            P(None, ("cuts", "stem"), None, None),
        ),
        out_specs=P("cuts"),
        check_vma=False,
    )
```

```python
import functools

import jax
import jax.numpy as jnp
from jax import lax
from jax.experimental import pallas as pl
from jax.experimental.pallas import tpu as pltpu
from jax.sharding import PartitionSpec as P

MESH = pl.DeviceIdType.MESH
NX = 4
NCORE = 2


def tree_sum(values):
    while len(values) > 1:
        odd = values[len(values) // 2 * 2:]
        values = [a + b for a, b in zip(values[::2], values[1::2])] + odd
    return values[0]


def kernel(
    nz, ny,
    stem_hbm, mid_hbm, right_hbm, out_ref,
    stem_v, mid_v, right_v, rhs_v, lhs_v, mix_v, acc_v, send1, recv1, send2, recv2,
    stem_sem, mid_sem, right_sem, gs_send, gs_recv, r_send, r_recv, round_sem,
):
    cut, y = lax.axis_index("cuts"), lax.axis_index("stem")
    core = lax.rem(cut, NCORE)
    x = lax.rem(lax.div(cut, NCORE), NX)
    z = lax.div(cut, NCORE * NX)
    plane = NX * NCORE * ny
    parts = NCORE * ny
    part = y * NCORE + core
    per = nz // parts
    xs = [lax.rem(x + d, NX) for d in range(NX)]
    ys = [lax.rem(y + d, ny) for d in range(ny)]
    cores = [core, 1 - core]

    def hops(d, n):
        return min(d, n - d)

    def signal(device):
        pl.semaphore_signal(barrier, inc=1, device_id=device, device_id_type=MESH)

    def at(z_, x_, core_):
        return (z_ * NX + x_) * NCORE + core_

    blocks = stem_hbm.shape[0]
    load_stem = pltpu.make_async_copy(stem_hbm, stem_v.at[pl.ds(y * blocks, blocks)], stem_sem)
    load_stem.start()

    barrier = pltpu.get_barrier_semaphore()

    def zs(d):
        return (at(lax.rem(z + d, nz), x, core), y)

    near = [(cut, ys[1]), (cut, ys[ny - 1]), (at(z, x, cores[1]), y)]
    near += [(at(z, xs[d], core), y) for d in (1, NX - 1)] + [zs(d) for d in (1, nz - 1)]
    for device in near:
        signal(device)

    rounds = [
        near,
        [(at(z, xs[2], core), y), (cut, ys[2]), zs(2), zs(nz - 2)],
        [(at(z, x, cores[1]), y), zs(4), zs(nz - 4)],
    ]

    def announce(n):
        for device in rounds[n]:
            pl.semaphore_signal(round_sem.at[n], inc=1, device_id=device, device_id_type=MESH)

    def heard(n):
        pl.semaphore_wait(round_sem.at[n], len(rounds[n]))

    load_mid = pltpu.make_async_copy(mid_hbm, mid_v, mid_sem)
    load_right = pltpu.make_async_copy(right_hbm, right_v, right_sem)
    load_mid.start()
    load_right.start()
    pl.semaphore_wait(barrier, len(near))

    rows = stem_hbm.shape[1]
    half = rows // 2
    up, far, down = ys[1], ys[2], ys[3]
    other = at(z, x, cores[1])

    def piece(y_, h):
        return stem_v.at[y_ * blocks + core, pl.ds(h * half, half)]

    def push(n, src, dst, device):
        return pltpu.make_async_remote_copy(
            src_ref=src, dst_ref=dst, send_sem=gs_send.at[n], recv_sem=gs_recv.at[n],
            device_id=device, device_id_type=MESH,
        )

    load_stem.wait()
    mine = [piece(y, 0), piece(y, 1)]
    arriving = [
        push(0, mine[0], piece(y, 0), (cut, up)),
        push(1, mine[1], piece(y, 1), (cut, down)),
        push(2, mine[1], piece(y, 1), (cut, up)),
        push(3, mine[0], piece(y, 0), (cut, down)),
        push(4, piece(down, 0), piece(down, 0), (cut, up)),
        push(5, piece(up, 1), piece(up, 1), (cut, down)),
    ]
    for copy in arriving[:4]:
        copy.start()

    announce(0)
    arrived = [piece(down, 0), piece(up, 1), piece(down, 1), piece(up, 0), piece(far, 0), piece(far, 1)]
    shared = [push(6 + n, arrived[n], arrived[n], (other, y)) for n in range(6)]

    def pass_on(n):
        arriving[n].wait_recv()
        arriving[4 + n].start()

    def share(*which):
        for n in which:
            arriving[n].wait_recv()
            shared[n].start()

    depth, width = mid_hbm.shape[1:]
    r = width // 2
    load_mid.wait()
    for p in range(mid_hbm.shape[0] // 2):
        a, b = mid_v[2 * p], mid_v[2 * p + 1]
        rhs_v[0:depth, p * width:(p + 1) * width] = jnp.concatenate([a[:, :r], b[:, :r]], axis=1)
        rhs_v[depth:, p * width:(p + 1) * width] = jnp.concatenate([a[:, r:], b[:, r:]], axis=1)

    tile = 256

    def contract(slot, y_, core_, start=False):
        s = stem_v[y_ * blocks + core_]
        re, im = s[:, :depth], s[:, depth:]
        lhs_v[slot, :rows, :depth] = re
        lhs_v[slot, :rows, depth:] = -im
        lhs_v[slot, rows:, :depth] = im
        lhs_v[slot, rows:, depth:] = re
        for n in range(rhs_v.shape[1] // tile):
            mix_v[slot, :, n * tile:(n + 1) * tile] = jnp.dot(
                lhs_v[slot], rhs_v[:, n * tile:(n + 1) * tile], preferred_element_type=jnp.float32
            ).astype(jnp.bfloat16)
        if start:
            load_right.wait()
        update = jnp.dot(mix_v[slot], right_v[y_ * blocks + core_], preferred_element_type=jnp.float32)
        acc_v[...] = update if start else acc_v[...] + update

    heard(0)
    announce(1)
    contract(0, y, cores[0], start=True)
    contract(1, y, cores[1])
    pass_on(0)
    pass_on(1)
    for n in (0, 1):
        shared[n].start()
    heard(1)
    announce(2)
    share(2, 3)
    contract(0, down, cores[0])
    contract(1, up, cores[0])
    for n in (0, 2):
        shared[n].wait_recv()
    contract(0, down, cores[1])
    for n in (1, 3):
        shared[n].wait_recv()
    contract(1, up, cores[1])
    share(4, 5)
    contract(0, far, cores[0])
    for n in (4, 5):
        shared[n].wait_recv()
    contract(1, far, cores[1])

    heard(2)
    top, bottom = acc_v[0:rows], acc_v[rows:]
    turned = pltpu.roll(bottom, r, axis=1)
    lane = lax.broadcasted_iota(jnp.int32, turned.shape, 1)
    total = top + jnp.where(lane < r, -turned, turned)
    place = x * parts + part

    def send(part_, x_):
        pltpu.make_async_remote_copy(
            src_ref=send1.at[part_ * NX + x_], dst_ref=recv1.at[place],
            send_sem=r_send.at[0], recv_sem=r_recv.at[0],
            device_id=(at(z, x_, part_ % NCORE), part_ // NCORE), device_id_type=MESH,
        ).start()

    for part_ in range(parts):
        for x_ in range(NX):
            for k in range(per):
                row = (part_ * per + k) * NX + x_
                send1[part_ * NX + x_, k:k + 1, :] = total[row:row + 1]
        for x_ in range(NX):
            pl.when(place != x_ * parts + part_)(functools.partial(send, part_, x_))
    recv1[place] = send1[part * NX + x]
    all1 = pltpu.make_async_remote_copy(
        src_ref=send1.at[pl.ds(0, plane - 1)], dst_ref=recv1.at[pl.ds(0, plane - 1)],
        send_sem=r_send.at[0], recv_sem=r_recv.at[0], device_id=(cut, y), device_id_type=MESH,
    )
    all1.wait_recv()
    sums = tree_sum([recv1[n] for n in range(plane)])
    for k in range(per):
        send2[k] = sums[k:k + 1]

    def deliver(k, device):
        pltpu.make_async_remote_copy(
            src_ref=send2.at[k], dst_ref=recv2.at[z],
            send_sem=r_send.at[1], recv_sem=r_recv.at[1], device_id=device, device_id_type=MESH,
        ).start()

    for k in range(per):
        for dy in sorted(range(ny), key=lambda d: hops(d, ny)):
            for dc in reversed(range(NCORE)):
                z_ = part * per + k
                device = (at(z_, x, cores[dc]), ys[dy])
                if dy or dc:
                    deliver(k, device)
                else:
                    pl.when(z_ != z)(functools.partial(deliver, k, device))

                    @pl.when(z_ == z)
                    def _():
                        recv2[z] = send2[k]

    in_own = lax.div(z, per) == part

    def all2(n):
        return pltpu.make_async_remote_copy(
            src_ref=recv2.at[pl.ds(0, n)], dst_ref=recv2.at[pl.ds(0, n)],
            send_sem=r_send.at[1], recv_sem=r_recv.at[1], device_id=(cut, y), device_id_type=MESH,
        )

    @pl.when(in_own)
    def _():
        all2(nz - 1).wait_recv()

    @pl.when(jnp.logical_not(in_own))
    def _():
        all2(nz).wait_recv()

    out_ref[...] = tree_sum([recv2[n] for n in range(nz)])

    for copy in arriving + shared:
        copy.wait_send()
    all1.wait_send()

    @pl.when(in_own)
    def _():
        all2(nz - 1).wait_send()

    @pl.when(jnp.logical_not(in_own))
    def _():
        all2(nz).wait_send()


def on_device(nz, ny, stem_tensor, mid_tensors, right_tensors):
    blocks, rows, width = stem_tensor.shape
    terms, pairs, r, cols = right_tensors.shape
    depth = mid_tensors.shape[1]
    plane = NX * NCORE * ny
    per = nz // (NCORE * ny)
    anywhere = pl.BlockSpec(memory_space=pl.ANY)
    out = pl.pallas_call(
        functools.partial(kernel, nz, ny),
        out_shape=pltpu.VMEM((1, cols), jnp.float32),
        in_specs=[anywhere] * 3,
        out_specs=pl.BlockSpec(memory_space=pltpu.VMEM),
        scratch_shapes=[
            pltpu.VMEM((terms, rows, width), jnp.bfloat16),
            pltpu.VMEM(mid_tensors.shape, jnp.bfloat16),
            pltpu.VMEM((terms, pairs * r, cols), jnp.bfloat16),
            pltpu.VMEM((2 * depth, pairs * r), jnp.bfloat16),
            pltpu.VMEM((2, 2 * rows, width), jnp.bfloat16),
            pltpu.VMEM((2, 2 * rows, pairs * r), jnp.bfloat16),
            pltpu.VMEM((2 * rows, cols), jnp.float32),
            pltpu.VMEM((plane, per, cols), jnp.float32),
            pltpu.VMEM((plane, per, cols), jnp.float32),
            pltpu.VMEM((per, 1, cols), jnp.float32),
            pltpu.VMEM((nz, 1, cols), jnp.float32),
            pltpu.SemaphoreType.DMA,
            pltpu.SemaphoreType.DMA,
            pltpu.SemaphoreType.DMA,
            pltpu.SemaphoreType.DMA((12,)),
            pltpu.SemaphoreType.DMA((12,)),
            pltpu.SemaphoreType.DMA((2,)),
            pltpu.SemaphoreType.DMA((2,)),
            pltpu.SemaphoreType.REGULAR((3,)),
        ],
        compiler_params=pltpu.CompilerParams(
            collective_id=0, has_side_effects=True, vmem_limit_bytes=60 * 2**20
        ),
    )(stem_tensor, mid_tensors, right_tensors.reshape(terms, pairs * r, cols))
    portion = cols // NCORE
    start = lax.rem(lax.axis_index("cuts"), NCORE) * portion
    return lax.dynamic_slice_in_dim(out.reshape(-1), start, portion)


def solution(mesh):
    return jax.shard_map(
        functools.partial(on_device, mesh.shape["cuts"] // (NX * NCORE), mesh.shape["stem"]),
        mesh=mesh,
        in_specs=(
            P("stem", None, None),
            P(("cuts", "stem"), None, None),
            P(None, ("cuts", "stem"), None, None),
        ),
        out_specs=P("cuts"),
        check_vma=False,
    )
```
